32 devices in a mesh: row: 16 (over z, y, core), col: 2 (over x).
Axes of the slice: x: 2, y: 2, z: 4, core: 2. Of those that a mesh axis runs over, the one named last changes fastest.
Arguments:
- blocks: bfloat16 [32768, 4096], P('row', 'col'), may hold values from -0.046875 to 0.046875
- factors: float32 [64, 512, 512], P('row'), as said below
- block_live: int32 [64], P('row'), may hold values from 1 to 512, 24576 in all
Outputs:
- schur_matrix: float32 [4096, 4096], P('row', 'col')
- panel_factor: float32 [4096, 512], P('row', 'col')
The draws below stay inside these ranges and needn't reach their ends.
Inputs may be any that keep to these rules, and one draw needn't show every extreme that they name: `factors`: each block is lower triangular with a positive diagonal and zeros above it. `block_live`: rows of a block at or beyond its count are left out.
All inputs are finite; a program needn't handle non-finite values.
Results may differ from the reference program's by a relative error of at most 0.0014.
Values may be sent and summed in bfloat16 or wider, within the bound.
No kernel may reach another device: no remote copies, remote signals or barrier semaphores. Data moves between devices by JAX's collectives and lax.ppermute only.
A program may use at most 128 MiB of HBM per device.

```python
import math
import jax
import jax.numpy as jnp
import numpy as np
from jax import lax

N = 4096
BLK = 512
LEAD = 512
BLOCKS = 64
P_SIZE = 32768


def draw_factors(key, part):
    first_key, second_key = jax.random.split(jax.random.fold_in(key, 17))
    strict = jax.random.normal(first_key, (BLOCKS, BLK, BLK), jnp.float32) * (0.5 / math.sqrt(BLK))
    strict = jnp.tril(strict, -1)
    diagonal = jax.random.uniform(second_key, (BLOCKS, BLK), jnp.float32, 1.0, 2.0)
    return strict + jnp.eye(BLK, dtype=jnp.float32)[None, :, :] * diagonal[:, :, None]


def strengthened(entries, rng, source, target, parts, factor):
    def block_of(axis_at):
        return (jnp.arange(entries.shape[axis_at]) // (entries.shape[axis_at] // parts)).reshape((-1,) + (1,) * (entries.ndim - 1 - axis_at))

    near = jax.random.permutation(rng, parts)[block_of(target)]
    far = (block_of(target) + parts // 2) % parts
    return jnp.where((block_of(source) == near) | (block_of(source) == far), factor * entries, entries)


def levels(own_key, extent, cuts, low, largest):
    def one(dim, blocks):
        draws = jax.random.uniform(jax.random.fold_in(jax.random.fold_in(own_key, 6), dim), (blocks,), jnp.float32, low / len(cuts), largest / len(cuts))
        return jnp.repeat(jnp.exp(draws), extent[dim] // blocks).reshape((-1,) + (1,) * (len(extent) - dim - 1))

    factor_of = one(*cuts[0])
    for cut in cuts[1:]:
        factor_of = factor_of * one(*cut)
    return factor_of


def split_up(number_of, total, reach, slope):
    loads = [(1 << 20) // math.isqrt(standing ** slope) + 1 for standing in range(2, number_of + 1)]
    rest, counts = total - reach - (number_of - 1), [1] * (number_of - 1)
    while rest > 0:
        movable = [i for i in range(number_of - 1) if counts[i] < reach]
        mass, remaining = sum([loads[i] for i in movable]), rest
        for i in movable:
            extra = min(reach - counts[i], max(1, remaining * loads[i] // mass), rest)
            counts[i] = counts[i] + extra
            rest = rest - extra
    return np.array([reach] + counts)


def ragged(own_key, number_of, total, reach, skew):
    if number_of == 2:
        one = jax.random.randint(own_key, (), max(1, total - reach), min(reach, total - 1) + 1)
        return jnp.stack([one, total - one])
    tallies = jnp.asarray(split_up(number_of, total, reach, skew), jnp.int32)
    pairs = (number_of - 1) // 2
    donor, taker = tallies[1:1 + 2 * pairs:2], tallies[2:2 + 2 * pairs:2]
    room = jnp.minimum(donor - 1, reach - taker)
    passed = jax.random.randint(jax.random.fold_in(own_key, 1), (pairs,), 0, 1 << 20) % (room + 1)
    tallies = tallies.at[1:1 + 2 * pairs:2].set(donor - passed).at[2:2 + 2 * pairs:2].set(taker + passed)
    return tallies[jax.random.permutation(jax.random.fold_in(own_key, 2), number_of)]


def bell_draw_with(key, extent, spread, bound, pieces, heavy, kind=jnp.bfloat16):
    drawn = spread * jax.random.normal(key, extent, jnp.float32)
    if pieces:
        drawn = drawn * levels(key, extent, pieces, -0.22, 0.18)
    return jnp.clip(strengthened(drawn, jax.random.fold_in(key, 3), *heavy), -bound, bound).astype(kind)


def setup_inputs(seed: int = 0) -> dict:
    streams_of = jax.random.split(jax.random.key(seed), 4)
    return {
        "blocks": bell_draw_with(streams_of[0], (P_SIZE, N), P_SIZE ** -0.5, 0.046875, ((0, 16), (1, 2)), (0, 1, 16, 2.0)),
        "factors": draw_factors(jax.random.fold_in(streams_of[3], 71), 0),
        "block_live": ragged(streams_of[2], BLOCKS, 3 * BLOCKS * BLK // 4, BLK, 1).astype(jnp.int32),
    }


def reference(blocks, factors, block_live):
    columns = blocks.shape[1]
    shaped = blocks.reshape(BLOCKS, BLK, columns)
    row_index = jnp.arange(BLK, dtype=jnp.int32)

    def accumulate(running, inputs):
        factor, segment, live_rows = inputs
        solved = jax.scipy.linalg.solve_triangular(factor, segment.astype(jnp.float32), lower=True)
        solved = jnp.where(row_index[:, None] < live_rows, solved, 0.0).astype(jnp.bfloat16)
        solved = lax.optimization_barrier(solved)
        widened = solved.astype(jnp.float32)
        return (running + jnp.dot(widened.T, widened, precision=lax.Precision.HIGHEST), None)
    schur_matrix, _ = lax.scan(accumulate, jnp.zeros((columns, columns), jnp.float32), (factors, shaped, block_live))
    leading_block = schur_matrix[:LEAD, :LEAD]
    lead_factor = jnp.linalg.cholesky(leading_block)
    lead_inverse = jax.scipy.linalg.solve_triangular(lead_factor, jnp.eye(LEAD, dtype=jnp.float32), lower=True)
    panel_factor = jnp.dot(schur_matrix[:, :LEAD], lead_inverse.T, precision=lax.Precision.HIGHEST)
    return (schur_matrix, panel_factor)
```

```python
import functools

import jax
import jax.numpy as jnp
from jax import lax
from jax.experimental import pallas as pl
from jax.experimental.pallas import tpu as pltpu
from jax.sharding import PartitionSpec as P

LEAD = 512
TILE = 128
BASE = 8
COLUMN_PARTS = 2
F32 = jnp.float32
BF16 = jnp.bfloat16


def dot32(a, b):
    a_hi, b_hi = a.astype(BF16), b.astype(BF16)
    a_lo = (a - a_hi.astype(F32)).astype(BF16)
    b_lo = (b - b_hi.astype(F32)).astype(BF16)
    dot = functools.partial(jnp.dot, preferred_element_type=F32)
    return dot(a_hi, b_hi) + (dot(a_hi, b_lo) + dot(a_lo, b_hi))


def invert_tile(tile):
    order = tile.shape[0]
    row = lax.broadcasted_iota(jnp.int32, (order, order), 0)
    col = lax.broadcasted_iota(jnp.int32, (order, order), 1)
    near = row // BASE == col // BASE
    groups = (order // BASE, BASE, order)
    inverse = jnp.where(row == col, 1.0, 0.0).astype(F32).reshape(groups)
    inner = lax.broadcasted_iota(jnp.int32, groups, 1)
    for k in range(BASE):
        picked = jnp.where(near & (col % BASE == k), tile, 0.0)
        coefficient = jnp.sum(picked, axis=1, keepdims=True).reshape(order // BASE, BASE, 1)
        solved = inverse[:, k : k + 1, :] / coefficient[:, k : k + 1, :]
        inverse = jnp.where(
            inner == k, solved, jnp.where(inner > k, inverse - coefficient * solved, inverse)
        )
    inverse = inverse.reshape(order, order)
    size = BASE
    while size < order:
        below = (row // (2 * size) == col // (2 * size)) & (row // size != col // size)
        coupling = jnp.where(below & (row > col), tile, 0.0)
        inverse = inverse - dot32(inverse, dot32(coupling, inverse))
        size *= 2
    return inverse


def invert_lower(read, work, order):
    work[...] = jnp.zeros_like(work)
    for t in range(order // TILE):
        at = slice(t * TILE, (t + 1) * TILE)
        work[at, at] = invert_tile(read(at, at))
    size = TILE
    while size < order:
        for start in range(0, order, 2 * size):
            top = slice(start, start + size)
            low = slice(start + size, start + 2 * size)
            work[low, top] = -dot32(work[low, low], dot32(read(low, top), work[top, top]))
        size *= 2


def invert_kernel(factor, hi, lo, work):
    invert_lower(lambda r, c: factor[0, r, c], work, factor.shape[1])
    value = work[...]
    rounded = value.astype(BF16)
    hi[0] = rounded
    lo[0] = (value - rounded.astype(F32)).astype(BF16)


def invert_factors(factors):
    count, order, _ = factors.shape
    spec = pl.BlockSpec((1, order, order), lambda b: (b, 0, 0))
    return pl.pallas_call(
        invert_kernel,
        grid=(count,),
        in_specs=[spec],
        out_specs=[spec, spec],
        out_shape=[jax.ShapeDtypeStruct(factors.shape, BF16)] * 2,
        scratch_shapes=[pltpu.VMEM((order, order), F32)],
        name="invert_factors",
    )(factors)


def dot32_nt(a, b):
    a_hi, b_hi = a.astype(BF16), b.astype(BF16)
    a_lo = (a - a_hi.astype(F32)).astype(BF16)
    b_lo = (b - b_hi.astype(F32)).astype(BF16)

    def dot(x, y):
        return lax.dot_general(x, y, (((1,), (1,)), ((), ())), preferred_element_type=F32)

    return dot(a_hi, b_hi) + (dot(a_hi, b_lo) + dot(a_lo, b_hi))


def eliminate_tile(tile):
    row = lax.broadcasted_iota(jnp.int32, (8, TILE), 0)
    col = lax.broadcasted_iota(jnp.int32, (8, TILE), 1)
    count = TILE // 8
    left = [tile[8 * g : 8 * g + 8] for g in range(count)]
    right = [jnp.where(col == row + 8 * g, 1.0, 0.0).astype(F32) for g in range(count)]
    for k in range(TILE):
        at, inside = k // 8, k % 8
        pivot_row = left[at][inside : inside + 1]
        pivot_right = right[at][inside : inside + 1]
        inverse = 1.0 / pivot_row[:, k : k + 1]
        scaled, scaled_right = pivot_row * inverse, pivot_right * inverse
        for g in range(at, count):
            factor = left[g][:, k : k + 1]
            if g == at:
                factor = jnp.where(row[:, :1] > inside, factor, 0.0)
            left[g] = left[g] - factor * scaled
            right[g] = right[g] - factor * scaled_right
    out = []
    for g in range(count):
        pivot = jnp.sum(jnp.where(col == row + 8 * g, left[g], 0.0), axis=1, keepdims=True)
        out.append(right[g] / jnp.sqrt(pivot))
    return jnp.concatenate(out, axis=0)


def lead_inverse_kernel(tiles, out, work):
    order = out.shape[0]
    t = 0
    for i in range(order // TILE):
        for k in range(i + 1):
            work[i * TILE : (i + 1) * TILE, k * TILE : (k + 1) * TILE] = tiles[t]
            t += 1
    row = lax.broadcasted_iota(jnp.int32, (order, order), 0)
    col = lax.broadcasted_iota(jnp.int32, (order, order), 1)
    out[...] = jnp.where(row == col, 1.0, 0.0).astype(F32)
    panel_row = lax.broadcasted_iota(jnp.int32, (order, TILE), 0)

    def step(j, _):
        at = pl.ds(pl.multiple_of(j * TILE, TILE), TILE)
        inverse = eliminate_tile(work[at, at])
        mine = dot32(inverse, out[at, :])
        panel = jnp.where(panel_row >= (j + 1) * TILE, dot32_nt(work[:, at], inverse), 0.0)
        work[...] -= dot32_nt(panel, panel)
        out[...] -= dot32(panel, mine)
        out[at, :] = mine
        return 0

    for i in range(order // TILE):
        for k in range(i + 1, order // TILE):
            work[i * TILE : (i + 1) * TILE, k * TILE : (k + 1) * TILE] = jnp.zeros((TILE, TILE), F32)
    lax.fori_loop(0, order // TILE, step, 0)


def invert_lead(tiles, order):
    return pl.pallas_call(
        lead_inverse_kernel,
        out_shape=jax.ShapeDtypeStruct((order, order), F32),
        scratch_shapes=[pltpu.VMEM((order, order), F32)],
        name="invert_lead",
    )(tiles)


def pick_kernel(source, out):
    out[...] = source[...]


def pick(blocks, groups, pieces, piece):
    rows = blocks.shape[0]
    return pl.pallas_call(
        pick_kernel,
        grid=(groups,),
        in_specs=[pl.BlockSpec((rows, TILE), lambda g: (0, g * pieces + piece))],
        out_specs=pl.BlockSpec((rows, TILE), lambda g: (0, g)),
        out_shape=jax.ShapeDtypeStruct((rows, groups * TILE), blocks.dtype),
        name="pick",
    )(blocks)


def whiten_kernel(slab, live, place, hi, lo, raw, moved, *rest):
    b = pl.program_id(0)
    order, columns = raw.shape
    keep = lax.broadcasted_iota(jnp.int32, (order, slab), 0) < live[b]
    if rest:
        natural, norms = rest

        @pl.when(b == 0)
        def _():
            norms[...] = jnp.zeros_like(norms)

    for s in range(columns // slab):
        at = slice(s * slab, (s + 1) * slab)
        part = raw[:, at]
        solved = jnp.dot(hi[0], part, preferred_element_type=F32) + jnp.dot(
            lo[0], part, preferred_element_type=F32
        )
        value = jnp.where(keep, solved, 0.0).astype(BF16)
        moved[:, pl.ds(pl.multiple_of(place[s] * slab, TILE), slab)] = value
        if rest:
            natural[:, at] = value
            wide = value.astype(F32)
            norms[:, at] += jnp.sum((wide * wide).reshape(order // 8, 8, slab), axis=0)


def whiten(hi, lo, raw, block_live, place, slab, own):
    count, order, _ = hi.shape
    columns = raw.shape[1]
    factor_spec = pl.BlockSpec((1, order, order), lambda b, *_: (b, 0, 0))
    data_spec = pl.BlockSpec((order, columns), lambda b, *_: (b, 0))
    out_specs = [data_spec]
    out_shape = [jax.ShapeDtypeStruct(raw.shape, BF16)]
    if own:
        out_specs += [data_spec, pl.BlockSpec((8, columns), lambda b, *_: (0, 0))]
        out_shape += [jax.ShapeDtypeStruct(raw.shape, BF16), jax.ShapeDtypeStruct((8, columns), F32)]
    return pl.pallas_call(
        functools.partial(whiten_kernel, slab),
        grid_spec=pltpu.PrefetchScalarGridSpec(
            num_scalar_prefetch=2,
            grid=(count,),
            in_specs=[factor_spec, factor_spec, data_spec],
            out_specs=out_specs,
        ),
        out_shape=out_shape,
        name="whiten_own" if own else "whiten_other",
    )(block_live, place, hi, lo, raw)


def gram(left, right):
    return lax.dot_general(left, right, (((0,), (0,)), ((), ())), preferred_element_type=F32)


def body(blocks, factors, block_live):
    rows, cols = lax.axis_size("row"), lax.axis_size("col")
    my_row, my_col = lax.axis_index("row"), lax.axis_index("col")
    width = blocks.shape[1]
    slab = width * cols // rows
    groups = rows // cols
    low_bits = groups.bit_length() - 1
    row_bits = rows.bit_length() - 1

    def flip_send(value, bit, step=None):
        pairs = []
        for r in range(rows):
            for c in range(cols):
                if step is not None:
                    goal = (c - step) % cols
                    settled = (1 << (bit - low_bits)) - 1
                    here = r >> low_bits
                    if (here ^ goal) & settled or not ((here ^ goal) >> (bit - low_bits)) & 1:
                        continue
                pairs.append((r * cols + c, (r ^ (1 << bit)) * cols + c))
        return lax.ppermute(value, ("row", "col"), pairs)

    def reduced(left, right, step, marks=None):
        half = left.shape[1] // 2
        received = flip_send(gram(left[:, half:], right).astype(BF16), 0)
        total = gram(left[:, :half], right) + received.astype(F32)
        if marks is not None:
            marks.append(total)
        for bit in range(1, low_bits):
            half //= 2
            received = flip_send(total[half:].astype(BF16), bit)
            total = total[:half] + received.astype(F32)
        for bit in range(low_bits, row_bits):
            total = total + flip_send(total.astype(BF16), bit, step).astype(F32)
        return total

    index = jnp.arange(groups, dtype=jnp.int32) ^ (my_row % groups).astype(jnp.int32)
    place = jnp.zeros_like(index)
    for bit in range(low_bits):
        place = place | (((index >> bit) & 1) << (low_bits - 1 - bit))

    pieces = slab // TILE
    picked = [pick(blocks, groups, pieces, j) for j in range(pieces)] if pieces > 1 else [blocks]
    arriving = []
    for step in range(1, cols):
        ring = [(c, (c + step) % cols) for c in range(cols)]
        arriving.append([lax.ppermute(value, "col", ring) for value in picked])

    hi, lo = invert_factors(factors)
    moved, own, norms = whiten(hi, lo, blocks, block_live, place, slab, True)

    lead = gram(own[:, :LEAD], own[:, :LEAD])
    tiles = LEAD // TILE
    lower = [
        lead[i * TILE : (i + 1) * TILE, k * TILE : (k + 1) * TILE]
        for i in range(tiles)
        for k in range(i + 1)
    ]
    extra = jnp.sum(norms, axis=0).reshape(-1, TILE)
    summed = lax.psum(jnp.concatenate(lower + [extra], axis=0), "row")
    diagonal = summed[len(lower) * TILE :].reshape(width)

    part_width = width // COLUMN_PARTS
    rights = [own[:, q * part_width : (q + 1) * part_width] for q in range(COLUMN_PARTS)]
    marks = []
    finished = [[reduced(moved, right, 0) for right in rights]]
    for step in range(1, cols):
        per_piece = []
        for raw in arriving[step - 1]:
            other = whiten(hi, lo, raw, block_live, place, TILE, False)[0]
            per_piece.append([reduced(other, right, step, marks) for right in rights])
        finished.append(
            [
                jnp.concatenate([piece[q] for piece in per_piece], axis=0)
                for q in range(COLUMN_PARTS)
            ]
        )

    lead_tiles = summed[: len(lower) * TILE].reshape(len(lower), TILE, TILE)
    lead_tiles, *_ = lax.optimization_barrier((lead_tiles, *marks[:COLUMN_PARTS]))
    lead_inverse = invert_lead(lead_tiles, LEAD)

    owner = my_row // groups
    row_at = (my_row % groups) * slab + lax.broadcasted_iota(jnp.int32, (slab, part_width), 0)
    slabs = []
    for q in range(COLUMN_PARTS):
        column_at = q * part_width + lax.broadcasted_iota(jnp.int32, (slab, part_width), 1)
        exact = diagonal[q * part_width : (q + 1) * part_width]
        value = jnp.where(row_at == column_at, exact[None, :], finished[0][q])
        for step in range(1, cols):
            value = jnp.where(owner == (my_col - step) % cols, finished[step][q], value)
        slabs.append(value)
    schur_slab = jnp.concatenate(slabs, axis=1)

    out_width = LEAD // cols
    leading = slabs[0] if part_width >= LEAD else schur_slab
    panel = jnp.dot(leading[:, :LEAD], lead_inverse.T, precision=lax.Precision.HIGHEST)
    panel_factor = panel[:, :out_width]
    for c in range(1, cols):
        sent = lax.ppermute(panel[:, c * out_width : (c + 1) * out_width], "col", [(0, c)])
        panel_factor = jnp.where(my_col == c, sent, panel_factor)
    return (schur_slab, panel_factor)


def solution(mesh):
    in_specs = (P("row", "col"), P("row", None, None), P("row"))
    out_specs = (P("row", "col"), P("row", "col"))
    return jax.shard_map(body, mesh=mesh, in_specs=in_specs, out_specs=out_specs, check_vma=False)
```

```python
import functools

import jax
import jax.numpy as jnp
from jax import lax
from jax.experimental import pallas as pl
from jax.experimental.pallas import tpu as pltpu
from jax.sharding import PartitionSpec as P


LEAD = 512
TILE = 128
BASE = 8
COLUMN_PARTS = 2
F32 = jnp.float32
BF16 = jnp.bfloat16


def dot32(a, b):
    a_hi, b_hi = a.astype(BF16), b.astype(BF16)
    a_lo = (a - a_hi.astype(F32)).astype(BF16)
    b_lo = (b - b_hi.astype(F32)).astype(BF16)
    dot = functools.partial(jnp.dot, preferred_element_type=F32)
    return dot(a_hi, b_hi) + (dot(a_hi, b_lo) + dot(a_lo, b_hi))


def invert_tile(tile):
    order = tile.shape[0]
    row = lax.broadcasted_iota(jnp.int32, (order, order), 0)
    col = lax.broadcasted_iota(jnp.int32, (order, order), 1)
    near = row // BASE == col // BASE
    groups = (order // BASE, BASE, order)
    inverse = jnp.where(row == col, 1.0, 0.0).astype(F32).reshape(groups)
    inner = lax.broadcasted_iota(jnp.int32, groups, 1)
    for k in range(BASE):
        picked = jnp.where(near & (col % BASE == k), tile, 0.0)
        coefficient = jnp.sum(picked, axis=1, keepdims=True).reshape(order // BASE, BASE, 1)
        solved = inverse[:, k : k + 1, :] / coefficient[:, k : k + 1, :]
        inverse = jnp.where(
            inner == k, solved, jnp.where(inner > k, inverse - coefficient * solved, inverse)
        )
    inverse = inverse.reshape(order, order)
    size = BASE
    while size < order:
        below = (row // (2 * size) == col // (2 * size)) & (row // size != col // size)
        coupling = jnp.where(below & (row > col), tile, 0.0)
        inverse = inverse - dot32(inverse, dot32(coupling, inverse))
        size *= 2
    return inverse


def invert_lower(read, work, order):
    work[...] = jnp.zeros_like(work)
    for t in range(order // TILE):
        at = slice(t * TILE, (t + 1) * TILE)
        work[at, at] = invert_tile(read(at, at))
    size = TILE
    while size < order:
        for start in range(0, order, 2 * size):
            top = slice(start, start + size)
            low = slice(start + size, start + 2 * size)
            work[low, top] = -dot32(work[low, low], dot32(read(low, top), work[top, top]))
        size *= 2


def invert_kernel(factor, hi, lo, work):
    invert_lower(lambda r, c: factor[0, r, c], work, factor.shape[1])
    value = work[...]
    rounded = value.astype(BF16)
    hi[0] = rounded
    lo[0] = (value - rounded.astype(F32)).astype(BF16)


def invert_factors(factors):
    count, order, _ = factors.shape
    spec = pl.BlockSpec((1, order, order), lambda b: (b, 0, 0))
    return pl.pallas_call(
        invert_kernel,
        grid=(count,),
        in_specs=[spec],
        out_specs=[spec, spec],
        out_shape=[jax.ShapeDtypeStruct(factors.shape, BF16)] * 2,
        scratch_shapes=[pltpu.VMEM((order, order), F32)],
        name="invert_factors",
    )(factors)


def dot32_nt(a, b):
    a_hi, b_hi = a.astype(BF16), b.astype(BF16)
    a_lo = (a - a_hi.astype(F32)).astype(BF16)
    b_lo = (b - b_hi.astype(F32)).astype(BF16)

    def dot(x, y):
        return lax.dot_general(x, y, (((1,), (1,)), ((), ())), preferred_element_type=F32)

    return dot(a_hi, b_hi) + (dot(a_hi, b_lo) + dot(a_lo, b_hi))


def eliminate_tile(tile):
    row = lax.broadcasted_iota(jnp.int32, (8, TILE), 0)
    col = lax.broadcasted_iota(jnp.int32, (8, TILE), 1)
    count = TILE // 8
    left = [tile[8 * g : 8 * g + 8] for g in range(count)]
    right = [jnp.where(col == row + 8 * g, 1.0, 0.0).astype(F32) for g in range(count)]
    for k in range(TILE):
        at, inside = k // 8, k % 8
        pivot_row = left[at][inside : inside + 1]
        pivot_right = right[at][inside : inside + 1]
        inverse = 1.0 / pivot_row[:, k : k + 1]
        scaled, scaled_right = pivot_row * inverse, pivot_right * inverse
        for g in range(at, count):
            factor = left[g][:, k : k + 1]
            if g == at:
                factor = jnp.where(row[:, :1] > inside, factor, 0.0)
            left[g] = left[g] - factor * scaled
            right[g] = right[g] - factor * scaled_right
    out = []
    for g in range(count):
        pivot = jnp.sum(jnp.where(col == row + 8 * g, left[g], 0.0), axis=1, keepdims=True)
        out.append(right[g] / jnp.sqrt(pivot))
    return jnp.concatenate(out, axis=0)


def lead_inverse_kernel(tiles, out, work):
    order = out.shape[0]
    t = 0
    for i in range(order // TILE):
        for k in range(i + 1):
            work[i * TILE : (i + 1) * TILE, k * TILE : (k + 1) * TILE] = tiles[t]
            t += 1
    row = lax.broadcasted_iota(jnp.int32, (order, order), 0)
    col = lax.broadcasted_iota(jnp.int32, (order, order), 1)
    out[...] = jnp.where(row == col, 1.0, 0.0).astype(F32)
    panel_row = lax.broadcasted_iota(jnp.int32, (order, TILE), 0)

    def step(j, _):
        at = pl.ds(pl.multiple_of(j * TILE, TILE), TILE)
        inverse = eliminate_tile(work[at, at])
        mine = dot32(inverse, out[at, :])
        panel = jnp.where(panel_row >= (j + 1) * TILE, dot32_nt(work[:, at], inverse), 0.0)
        work[...] -= dot32_nt(panel, panel)
        out[...] -= dot32(panel, mine)
        out[at, :] = mine
        return 0

    for i in range(order // TILE):
        for k in range(i + 1, order // TILE):
            work[i * TILE : (i + 1) * TILE, k * TILE : (k + 1) * TILE] = jnp.zeros((TILE, TILE), F32)
    lax.fori_loop(0, order // TILE, step, 0)


def invert_lead(tiles, order):
    return pl.pallas_call(
        lead_inverse_kernel,
        out_shape=jax.ShapeDtypeStruct((order, order), F32),
        scratch_shapes=[pltpu.VMEM((order, order), F32)],
        name="invert_lead",
    )(tiles)


def pick_kernel(source, out):
    out[...] = source[...]


def pick(blocks, groups, pieces, piece):
    rows = blocks.shape[0]
    return pl.pallas_call(
        pick_kernel,
        grid=(groups,),
        in_specs=[pl.BlockSpec((rows, TILE), lambda g: (0, g * pieces + piece))],
        out_specs=pl.BlockSpec((rows, TILE), lambda g: (0, g)),
        out_shape=jax.ShapeDtypeStruct((rows, groups * TILE), blocks.dtype),
        name="pick",
    )(blocks)


def whiten_kernel(slab, live, place, hi, lo, raw, moved, *rest):
    b = pl.program_id(0)
    order, columns = raw.shape
    keep = lax.broadcasted_iota(jnp.int32, (order, slab), 0) < live[b]
    if rest:
        natural, norms = rest

        @pl.when(b == 0)
        def _():
            norms[...] = jnp.zeros_like(norms)

    for s in range(columns // slab):
        at = slice(s * slab, (s + 1) * slab)
        part = raw[:, at]
        solved = jnp.dot(hi[0], part, preferred_element_type=F32) + jnp.dot(
            lo[0], part, preferred_element_type=F32
        )
        value = jnp.where(keep, solved, 0.0).astype(BF16)
        moved[:, pl.ds(pl.multiple_of(place[s] * slab, TILE), slab)] = value
        if rest:
            natural[:, at] = value
            wide = value.astype(F32)
            there = pl.ds(pl.multiple_of(place[s] * slab, TILE), slab)
            norms[:, there] += jnp.sum((wide * wide).reshape(order // 8, 8, slab), axis=0)


def whiten(hi, lo, raw, block_live, place, slab, own):
    count, order, _ = hi.shape
    columns = raw.shape[1]
    factor_spec = pl.BlockSpec((1, order, order), lambda b, *_: (b, 0, 0))
    data_spec = pl.BlockSpec((order, columns), lambda b, *_: (b, 0))
    out_specs = [data_spec]
    out_shape = [jax.ShapeDtypeStruct(raw.shape, BF16)]
    if own:
        out_specs += [data_spec, pl.BlockSpec((8, columns), lambda b, *_: (0, 0))]
        out_shape += [jax.ShapeDtypeStruct(raw.shape, BF16), jax.ShapeDtypeStruct((8, columns), F32)]
    return pl.pallas_call(
        functools.partial(whiten_kernel, slab),
        grid_spec=pltpu.PrefetchScalarGridSpec(
            num_scalar_prefetch=2,
            grid=(count,),
            in_specs=[factor_spec, factor_spec, data_spec],
            out_specs=out_specs,
        ),
        out_shape=out_shape,
        name="whiten_own" if own else "whiten_other",
    )(block_live, place, hi, lo, raw)


def lead_kernel(live, hi, lo, raw, tiles, total):
    b = pl.program_id(0)
    order, columns = raw.shape
    keep = lax.broadcasted_iota(jnp.int32, (order, columns), 0) < live[b]
    part = raw[...]
    solved = jnp.dot(hi[0], part, preferred_element_type=F32) + jnp.dot(
        lo[0], part, preferred_element_type=F32
    )
    value = jnp.where(keep, solved, 0.0).astype(BF16)
    product = lax.dot_general(value, value, (((0,), (0,)), ((), ())), preferred_element_type=F32)

    @pl.when(b == 0)
    def _():
        total[...] = product

    @pl.when(b > 0)
    def _():
        total[...] += product

    @pl.when(b == pl.num_programs(0) - 1)
    def _():
        t = 0
        for i in range(columns // TILE):
            for k in range(i + 1):
                tiles[t] = total[i * TILE : (i + 1) * TILE, k * TILE : (k + 1) * TILE]
                t += 1


def lead_gram(hi, lo, blocks, block_live):
    count, order, _ = hi.shape
    side = LEAD // TILE
    tiles = (side * (side + 1) // 2, TILE, TILE)
    factor_spec = pl.BlockSpec((1, order, order), lambda b, *_: (b, 0, 0))
    return pl.pallas_call(
        lead_kernel,
        grid_spec=pltpu.PrefetchScalarGridSpec(
            num_scalar_prefetch=1,
            grid=(count,),
            in_specs=[factor_spec, factor_spec, pl.BlockSpec((order, LEAD), lambda b, *_: (b, 0))],
            out_specs=pl.BlockSpec(tiles, lambda b, *_: (0, 0, 0)),
            scratch_shapes=[pltpu.VMEM((LEAD, LEAD), F32)],
        ),
        out_shape=jax.ShapeDtypeStruct(tiles, F32),
        name="lead_gram",
    )(block_live, hi, lo, blocks)


def gram(left, right):
    return lax.dot_general(left, right, (((0,), (0,)), ((), ())), preferred_element_type=F32)


def body(blocks, factors, block_live):
    rows, cols = lax.axis_size("row"), lax.axis_size("col")
    my_row, my_col = lax.axis_index("row"), lax.axis_index("col")
    width = blocks.shape[1]
    slab = width * cols // rows
    groups = rows // cols
    low_bits = groups.bit_length() - 1
    row_bits = rows.bit_length() - 1

    def flip_send(value, bit, step=None):
        pairs = []
        for r in range(rows):
            for c in range(cols):
                if step is not None:
                    goal = (c - step) % cols
                    settled = (1 << (bit - low_bits)) - 1
                    here = r >> low_bits
                    if (here ^ goal) & settled or not ((here ^ goal) >> (bit - low_bits)) & 1:
                        continue
                pairs.append((r * cols + c, (r ^ (1 << bit)) * cols + c))
        return lax.ppermute(value, ("row", "col"), pairs)

    def reduced(left, right, step, marks=None):
        half = left.shape[1] // 2
        received = flip_send(gram(left[:, half:], right).astype(BF16), 0)
        total = gram(left[:, :half], right) + received.astype(F32)
        if marks is not None:
            marks.append(total)
        for bit in range(1, low_bits):
            half //= 2
            sent = total[half:].astype(BF16)
            received = flip_send(sent, bit)
            total = total[:half] + received.astype(F32)
        for bit in range(low_bits, row_bits):
            total = total + flip_send(total.astype(BF16), bit, step).astype(F32)
        return total

    index = jnp.arange(groups, dtype=jnp.int32) ^ (my_row % groups).astype(jnp.int32)
    place = jnp.zeros_like(index)
    for bit in range(low_bits):
        place = place | (((index >> bit) & 1) << (low_bits - 1 - bit))

    pieces = slab // TILE
    rings = [[(c, (c + step) % cols) for c in range(cols)] for step in range(1, cols)]
    first = pick(blocks, groups, pieces, 0) if pieces > 1 else blocks
    factors, first = lax.optimization_barrier((factors, first))
    arriving = [[lax.ppermute(first, "col", ring)] for ring in rings]
    hi, lo = invert_factors(factors)
    tiles = lead_gram(hi, lo, blocks, block_live)
    lead_tiles = lax.psum(tiles, "row")
    if pieces > 1:
        later, tiles = lax.optimization_barrier((blocks, tiles))
        for j in range(1, pieces):
            value = pick(later, groups, pieces, j)
            for arrived, ring in zip(arriving, rings):
                arrived.append(lax.ppermute(value, "col", ring))

    blocks, _ = lax.optimization_barrier((blocks, tiles))
    moved, own, norms = whiten(hi, lo, blocks, block_live, place, slab, True)
    exact = jnp.sum(norms, axis=0).reshape(-1, TILE)
    for bit in range(low_bits):
        half = exact.shape[0] // 2
        exact = exact[:half] + flip_send(exact[half:], bit)
    for bit in range(low_bits, row_bits):
        exact = exact + flip_send(exact, bit, 0)
    exact = exact.reshape(slab)

    part_width = width // COLUMN_PARTS
    rights = [own[:, q * part_width : (q + 1) * part_width] for q in range(COLUMN_PARTS)]
    marks = []
    finished = [[reduced(moved, right, 0) for right in rights]]
    parts = [[] for _ in range(1, cols)]
    for j in range(pieces):
        for step in range(1, cols):
            raw = arriving[step - 1][j]
            if j == 1:
                raw, lead_inverse = lax.optimization_barrier((raw, lead_inverse))
            other = whiten(hi, lo, raw, block_live, place, TILE, False)[0]
            parts[step - 1].append([reduced(other, right, step, marks) for right in rights])
        if j == 0:
            lead_tiles, *_ = lax.optimization_barrier((lead_tiles, *marks))
            lead_inverse = invert_lead(lead_tiles, LEAD)
    for per_piece in parts:
        finished.append(
            [
                jnp.concatenate([piece[q] for piece in per_piece], axis=0)
                for q in range(COLUMN_PARTS)
            ]
        )

    owner = my_row // groups
    row_at = (my_row % groups) * slab + lax.broadcasted_iota(jnp.int32, (slab, part_width), 0)
    slabs = []
    for q in range(COLUMN_PARTS):
        column_at = q * part_width + lax.broadcasted_iota(jnp.int32, (slab, part_width), 1)
        value = jnp.where(row_at == column_at, exact[:, None], finished[0][q])
        for step in range(1, cols):
            value = jnp.where(owner == (my_col - step) % cols, finished[step][q], value)
        slabs.append(value)
    schur_slab = jnp.concatenate(slabs, axis=1)

    out_width = LEAD // cols
    leading = slabs[0] if part_width >= LEAD else schur_slab
    panel = jnp.dot(leading[:, :LEAD], lead_inverse.T, precision=lax.Precision.HIGHEST)
    panel_factor = panel[:, :out_width]
    for c in range(1, cols):
        sent = lax.ppermute(panel[:, c * out_width : (c + 1) * out_width], "col", [(0, c)])
        panel_factor = jnp.where(my_col == c, sent, panel_factor)
    return (schur_slab, panel_factor)


def solution(mesh):
    in_specs = (P("row", "col"), P("row", None, None), P("row"))
    out_specs = (P("row", "col"), P("row", "col"))
    return jax.shard_map(body, mesh=mesh, in_specs=in_specs, out_specs=out_specs, check_vma=False)
```
